32 devices in a mesh: groups: 2 (over y), seq: 16 (over z, x, core).
Axes of the slice: x: 2, y: 2, z: 4, core: 2. Of those that a mesh axis runs over, the one named last changes fastest.
Arguments:
- queries: bfloat16 [4, 32, 64, 3072], P('groups', 'seq'), parts along dimension 0, may hold values from -10 to 10
- own_kv: bfloat16 [4, 32, 64, 1024], P('groups', 'seq'), parts along dimension 0, may hold values from -10 to 10
- past_kv: bfloat16 [64, 16, 1024], P(('groups', 'seq')), parts along dimension 0, may hold values from -8 to 8
- block_home: int32 [64], P('groups'), parts along dimension 0, may hold values from 0 to 31, as said below
- block_list: int32 [32, 16], P('groups'), parts along dimension 0, may hold values from 0 to 31, as said below
- list_len: int32 [32], P('groups'), parts along dimension 0, may hold values from 1 to 16, as said below
- final_weight: bfloat16 [3072, 64], P('seq'), may hold values from -0.4375 to 0.4375
- decoder_weight: bfloat16 [432, 512], P(None, 'seq'), may hold values from -0.3125 to 0.3125
Outputs:
- features: bfloat16 [4, 64, 128, 512], P('groups', 'seq'), parts along dimension 0
The draws below stay inside these ranges and needn't reach their ends.
There are 2 independent parts, one for each index of `groups`. The reference program is written for one: setup_inputs(seed, part) draws one part's arguments, and reference() takes and returns one part's arrays. A program takes and returns all parts, laid end to end along the dimension named above; an argument that names none is the same for every part. Nothing has to cross between parts.
Inputs may be any that keep to these rules, and one draw needn't show every extreme that they name: Block i is stored at row block_home[i] of past_kv; every row holds one block. `block_list`: for each tile b the first list_len[b] entries name blocks stored by pairwise different devices (storage row // 2); later entries are not read. `list_len`: some tile lists 16 blocks.
All inputs are finite; a program needn't handle non-finite values.
Results may differ from the reference program's by a relative error of at most 0.0064.
Values may be sent and summed in bfloat16 or wider, within the bound.
A program may use at most 64 MiB of HBM per device.

```python
import math
import jax
import jax.numpy as jnp
from jax import lax

FRAMES = 2
WP = 64
HEADS = 24
KV_HEADS = 4
HEAD_DIM = 128
LAT = 16
CH = 512
BT = 16
BLK_DEV = 2
PROWS_ALL = 32
NB = 32
N_SEQ = 16


def segment_fields(key):
    folded = jax.random.fold_in(key, 7)
    query_shape = (FRAMES, PROWS_ALL, WP, HEADS * HEAD_DIM)
    key_shape = (FRAMES, PROWS_ALL, WP, 2 * KV_HEADS * HEAD_DIM)
    query_field = jnp.clip(1.4 * jax.random.normal(jax.random.fold_in(folded, 1), query_shape, jnp.float32), -8.0, 8.0)
    key_field = jnp.clip(1.4 * jax.random.normal(jax.random.fold_in(folded, 2), key_shape, jnp.float32), -8.0, 8.0)
    return (query_field, key_field)


def draw_queries(key, part):
    return segment_fields(key)[0].astype(jnp.bfloat16)


def draw_own_kv(key, part):
    return segment_fields(key)[1].astype(jnp.bfloat16)


def cache_tables(key):
    folded = jax.random.fold_in(key, 5)
    home_rows = jax.random.permutation(jax.random.fold_in(folded, 1), NB).astype(jnp.int32)
    stored_block = jnp.zeros((NB,), jnp.int32).at[home_rows].set(jnp.arange(NB, dtype=jnp.int32))
    row_keys = jax.random.split(jax.random.fold_in(folded, 2), N_SEQ)
    owners = jax.vmap(lambda subkey: jax.random.permutation(subkey, N_SEQ))(row_keys).astype(jnp.int32)
    local_index = jax.random.randint(jax.random.fold_in(folded, 3), (N_SEQ, N_SEQ), 0, BLK_DEV).astype(jnp.int32)
    chosen = stored_block[owners * BLK_DEV + local_index]
    counts = jax.random.randint(jax.random.fold_in(folded, 4), (N_SEQ,), 1, N_SEQ + 1).astype(jnp.int32)
    fullest = jax.random.randint(jax.random.fold_in(folded, 6), (), 0, N_SEQ).astype(jnp.int32)
    counts = jnp.where(jnp.arange(N_SEQ, dtype=jnp.int32) == fullest, N_SEQ, counts).astype(jnp.int32)
    return (home_rows, chosen, counts)


def draw_block_home(key, part):
    return cache_tables(key)[0]


def draw_block_list(key, part):
    return cache_tables(key)[1]


def draw_list_len(key, part):
    return cache_tables(key)[2]


def block_scale(own_key, extent, cuts, least, top_value):
    def one(axis_at, blocks):
        heights = jax.random.uniform(jax.random.fold_in(jax.random.fold_in(own_key, 6), axis_at), (blocks,), jnp.float32, least / len(cuts), top_value / len(cuts))
        return jnp.repeat(jnp.exp(heights), extent[axis_at] // blocks).reshape((-1,) + (1,) * (len(extent) - axis_at - 1))

    gain = one(*cuts[0])
    for cut in cuts[1:]:
        gain = gain * one(*cut)
    return gain


def scatter_about(stream_key, shape, width, reach, cuts=(), held_as=jnp.bfloat16):
    entries = jax.random.normal(stream_key, shape, jnp.float32) * width
    if len(cuts) > 0:
        entries = block_scale(stream_key, shape, cuts, -0.22, 0.18) * entries
    return jnp.clip(entries, min=-reach, max=reach).astype(held_as)


def setup_inputs(seed: int = 0, part: int = 0) -> dict:
    streams_of = jax.random.split(jax.random.key(seed), 9)
    part_keys = jax.random.split(jax.random.fold_in(streams_of[8], part), 9)
    return {
        "queries": draw_queries(jax.random.fold_in(jax.random.fold_in(streams_of[8], part), 71), part),
        "own_kv": draw_own_kv(jax.random.fold_in(jax.random.fold_in(streams_of[8], part), 71), part),
        "past_kv": scatter_about(part_keys[2], (NB, BT, 2 * KV_HEADS * HEAD_DIM), 1.4, 8.0, ((0, 16),)),
        "block_home": draw_block_home(jax.random.fold_in(jax.random.fold_in(streams_of[8], part), 71), part),
        "block_list": draw_block_list(jax.random.fold_in(jax.random.fold_in(streams_of[8], part), 71), part),
        "list_len": draw_list_len(jax.random.fold_in(jax.random.fold_in(streams_of[8], part), 71), part),
        "final_weight": scatter_about(streams_of[6], (HEADS * HEAD_DIM, 4 * LAT), (HEADS * HEAD_DIM // 16) ** -0.5, 0.4375, ((0, 16),)),
        "decoder_weight": scatter_about(streams_of[7], (27 * LAT, CH), (27 * LAT) ** -0.5, 0.3125, ((1, 16),)),
    }


def attend(query_rows, own_rows, past_rows, past_listed):
    tokens = query_rows.shape[0]
    group_size = HEADS // KV_HEADS
    key_width = KV_HEADS * HEAD_DIM
    score_scale = 1.0 / math.sqrt(HEAD_DIM)
    query_heads = query_rows.astype(jnp.float32).reshape(tokens, KV_HEADS, group_size, HEAD_DIM)
    keys_own = own_rows[:, :key_width].astype(jnp.float32).reshape(tokens, KV_HEADS, HEAD_DIM)
    values_own = own_rows[:, key_width:].astype(jnp.float32).reshape(tokens, KV_HEADS, HEAD_DIM)
    past_count = past_rows.shape[0]
    keys_past = past_rows[:, :key_width].astype(jnp.float32).reshape(past_count, KV_HEADS, HEAD_DIM)
    values_past = past_rows[:, key_width:].astype(jnp.float32).reshape(past_count, KV_HEADS, HEAD_DIM)
    scores_own = jnp.einsum('tkgd,skd->kgts', query_heads, keys_own) * score_scale
    scores_past = jnp.einsum('tkgd,skd->kgts', query_heads, keys_past) * score_scale
    scores_past = jnp.where(past_listed[None, None, None, :], scores_past, -1e+30)
    row_top = jnp.maximum(lax.optimization_barrier(jnp.max(scores_own, axis=-1, keepdims=True)), lax.optimization_barrier(jnp.max(scores_past, axis=-1, keepdims=True)))
    exp_own = jnp.exp(scores_own - row_top)
    exp_past = jnp.where(past_listed[None, None, None, :], jnp.exp(scores_past - row_top), 0.0)
    denominator = lax.optimization_barrier(jnp.sum(exp_own, axis=-1, keepdims=True)) + lax.optimization_barrier(jnp.sum(exp_past, axis=-1, keepdims=True))
    weights_own = lax.optimization_barrier((exp_own / denominator).astype(jnp.bfloat16)).astype(jnp.float32)
    weights_past = lax.optimization_barrier((exp_past / denominator).astype(jnp.bfloat16)).astype(jnp.float32)
    mixed = jnp.einsum('kgts,skd->tkgd', weights_own, values_own) + jnp.einsum('kgts,skd->tkgd', weights_past, values_past)
    return mixed.reshape(tokens, HEADS * HEAD_DIM).astype(jnp.bfloat16)

def reference(queries, own_kv, past_kv, block_home, block_list, list_len, final_weight, decoder_weight):
    frames, rows_all, patches, width_query = queries.shape
    tiles = N_SEQ
    patch_rows = rows_all // tiles
    tokens = frames * patch_rows * patches
    pair_width = own_kv.shape[3]

    def one_tile(tile_index):
        query_rows = lax.dynamic_slice_in_dim(queries, tile_index * patch_rows, patch_rows, 1).reshape(tokens, width_query)
        own_rows = lax.dynamic_slice_in_dim(own_kv, tile_index * patch_rows, patch_rows, 1).reshape(tokens, pair_width)
        stored_at = block_home[block_list[tile_index]]
        past_rows = past_kv[stored_at].reshape(tiles * BT, pair_width)
        listed = jnp.arange(tiles, dtype=jnp.int32) < list_len[tile_index]
        past_listed = jnp.repeat(listed, BT)
        return attend(query_rows, own_rows, past_rows, past_listed)
    attended = lax.map(one_tile, jnp.arange(tiles, dtype=jnp.int32))
    predicted = jnp.dot(attended.reshape(tiles * tokens, width_query), final_weight, preferred_element_type=jnp.float32).astype(jnp.bfloat16)
    latent_width = final_weight.shape[1] // 4
    latent = predicted.reshape(tiles, frames, patch_rows, patches, 2, 2, latent_width)
    latent = latent.transpose(1, 0, 2, 4, 3, 5, 6).reshape(frames, 2 * rows_all, 2 * patches, latent_width)
    padded = jnp.pad(latent, ((2, 0), (1, 1), (1, 1), (0, 0)))
    tall = 2 * rows_all
    broad = 2 * patches
    tap_list = []
    for shift_t in range(3):
        for shift_y in range(3):
            for shift_x in range(3):
                tap_list.append(padded[shift_t:shift_t + frames, shift_y:shift_y + tall, shift_x:shift_x + broad, :])
    columns = jnp.concatenate(tap_list, axis=3).reshape(frames * tall * broad, 27 * latent_width)
    features = jnp.dot(columns, decoder_weight, preferred_element_type=jnp.float32).astype(jnp.bfloat16)
    return features.reshape(frames, tall, broad, decoder_weight.shape[1])
```

```python
import functools
import math

import jax
import jax.numpy as jnp
from jax import lax
from jax.experimental import pallas as pl
from jax.experimental.pallas import tpu as pltpu
from jax.sharding import PartitionSpec as P

HEADS = 24
KV_HEADS = 4
HEAD_DIM = 128
GROUP = HEADS // KV_HEADS
CHUNK_SLOTS = 16
LOG2E = 1.0 / math.log(2.0)
SCALE = LOG2E / math.sqrt(HEAD_DIM)
ROWS = 2
BF = jnp.bfloat16
F32 = jnp.float32


def attend_kernel(
    shape,
    home_in, list_in, len_in, q_in, own_in, past_ref, final_ref, decoder_ref,
    taps, wd,
    pred_ref, lat, home_ref, list_ref, len_ref, q_ref, own_ref, fin_ref, dcd_ref, gp, gw, gd, kv, marks,
    acc, tops, attended, wf, rows_out, halo,
    load_sem, table_sem, send_sem, recv_sem, halo_send, halo_recv,
):
    n, outer, inner, blocks = shape
    me = lax.axis_index("seq")
    chip, core = me // 2, me % 2
    a, b = chip // inner, chip % inner
    key_width = KV_HEADS * HEAD_DIM
    tokens = q_ref.shape[0]
    slot_rows = gp.shape[2]
    width, panel = fin_ref.shape
    part, taps_all = dcd_ref.shape

    def device(ai, bi, ci):
        return (ai * inner + bi) * 2 + ci

    def across(i):
        if outer & (outer - 1):
            return (a + i) % outer
        at, bit = a, 1
        while bit < outer:
            if i & bit:
                at = at + bit - 2 * bit * ((a // bit) % 2)
            bit *= 2
        return at

    def source(i):
        return (a + outer - i) % outer if outer & (outer - 1) else across(i)

    pieces = blocks + 2

    def held(piece, slot):
        if piece < blocks:
            return gp.at[slot, piece]
        return (gw, gd)[piece - blocks].at[slot]

    loads = [
        pltpu.make_async_copy(past_ref.at[i], gp.at[me, i], load_sem.at[i])
        for i in range(blocks)
    ] + [
        pltpu.make_async_copy(final_ref, fin_ref, load_sem.at[blocks]),
        pltpu.make_async_copy(decoder_ref, dcd_ref, load_sem.at[blocks + 1]),
    ]
    for load in loads:
        load.start()
    tables = [
        pltpu.make_async_copy(ref, held_ref, table_sem.at[i])
        for i, (ref, held_ref) in enumerate(
            (
                (own_in, own_ref), (q_in, q_ref),
                (home_in, home_ref), (list_in, list_ref), (len_in, len_ref),
            )
        )
    ]
    for table in tables:
        table.start()

    partner = device(a, b, 1 - core)
    column = [device(across(i), b, core) for i in range(1, outer)]
    row = [device(a, (b + i) % inner, core) for i in range(1, inner)]
    barrier = pltpu.get_barrier_semaphore()
    around = [(me + 1) % n, (me + n - 1) % n]
    for peer in column + row + [partner] + around:
        pl.semaphore_signal(barrier, inc=1, device_id={"seq": peer})

    pl.semaphore_wait(barrier, outer + inner + 1)

    started = [[] for _ in range(pieces)]

    def send(piece, slot, target):
        copy = pltpu.make_async_remote_copy(
            src_ref=held(piece, slot),
            dst_ref=held(piece, slot),
            send_sem=send_sem.at[piece, len(started[piece])],
            recv_sem=recv_sem.at[piece, slot],
            device_id={"seq": target},
        )
        copy.start()
        started[piece].append(copy)

    def arrived(piece, slot):
        pltpu.make_async_remote_copy(
            src_ref=held(piece, slot),
            dst_ref=held(piece, slot),
            send_sem=send_sem.at[piece, 0],
            recv_sem=recv_sem.at[piece, slot],
            device_id={"seq": partner},
        ).wait_recv()

    def second(piece, i):
        slot = device(source(i), b, core)
        arrived(piece, slot)
        for peer in row:
            send(piece, slot, peer)
        send(piece, slot, partner)

    def third(piece, i):
        at = source(i) if i else a
        for j in range(1, inner):
            slot = device(at, (b + inner - j) % inner, core)
            arrived(piece, slot)
            send(piece, slot, partner)

    def last(piece, first, stop):
        for j in range(first, stop):
            for i in range(outer):
                arrived(piece, device((a + i) % outer, (b + j) % inner, 1 - core))

    past = range(blocks)
    weights_at = (blocks, blocks + 1)
    for piece in past:
        loads[piece].wait()
        for peer in column:
            send(piece, me, peer)
    for piece in past:
        for peer in row:
            send(piece, me, peer)
        send(piece, me, partner)

    def start_row(piece):
        for peer in row:
            send(piece, me, peer)
        send(piece, me, partner)

    def start_column(piece):
        for peer in column:
            send(piece, me, peer)

    def seconds(piece):
        for i in range(1, outer):
            second(piece, i)

    def thirds(piece, first=0):
        for i in range(first, outer):
            third(piece, i)

    loads[blocks].wait()
    loads[blocks + 1].wait()
    if gw.shape[1:] == (width, panel):
        gw[me] = fin_ref[...]
    else:
        gw[me, :width, :] = fin_ref[:, :HEAD_DIM]
        half = width // 2
        gw[me, width:, :] = jnp.concatenate(
            [fin_ref[:half, HEAD_DIM:], fin_ref[half:, HEAD_DIM:]], axis=1
        )
    gd[me] = dcd_ref[...]
    start_row(blocks)
    start_row(blocks + 1)

    def lanes(start):
        return pl.ds(pl.multiple_of(start, HEAD_DIM), HEAD_DIM)

    ones = jnp.ones((tokens, HEAD_DIM), BF)

    def wide(column):
        return jnp.broadcast_to(column, (tokens, HEAD_DIM))

    def weights(s, top):
        return jnp.concatenate(
            [
                jnp.exp2((s[:, i : i + HEAD_DIM] - top) * SCALE).astype(BF)
                for i in range(0, s.shape[1], HEAD_DIM)
            ],
            axis=1,
        )

    def own_part(start, stop):
        @pl.loop(start, stop)
        def _(g):
            keys = own_ref[:, lanes(g * HEAD_DIM)]
            values = jnp.concatenate(
                [own_ref[:, lanes(key_width + g * HEAD_DIM)], ones], axis=1
            )
            for i in range(GROUP):
                h = g * GROUP + i
                s = lax.dot_general(
                    q_ref[:, lanes(h * HEAD_DIM)], keys, (((1,), (1,)), ((), ())),
                    preferred_element_type=F32,
                )
                top = wide(jnp.max(s, axis=1, keepdims=True))
                acc[h] = jnp.dot(weights(s, top), values, preferred_element_type=F32)
                tops[h] = top

    frames, bordered, patches = pred_ref.shape[:3]
    lat_width = width // 4
    tall, broad = 2 * (bordered - 2), 2 * patches
    span = 3 * lat_width
    for f in range(frames):
        lat[f, :, 0:8, :] = jnp.zeros((tall + 2, 8, lat_width), F32)
        lat[f, :, 8 + broad : 16 + broad, :] = jnp.zeros((tall + 2, 8, lat_width), F32)
        for t in range(3):
            if f + t < 2:
                taps[f, :, :, 3 * t * span : 3 * (t + 1) * span] = jnp.zeros(
                    (tall, broad, 3 * span), BF
                )
    tables[0].wait()
    tables[1].wait()
    own_part(0, KV_HEADS)
    start_column(blocks)
    start_column(blocks + 1)
    for table in tables[2:]:
        table.wait()
    count = len_ref[me]
    chunks = list_ref.shape[1] // CHUNK_SLOTS

    def gather_chunk(c):
        for j in range(CHUNK_SLOTS):
            at = c * CHUNK_SLOTS + j
            listed = at < count
            entry = list_ref[me, jnp.where(listed, at, 0)]
            stored = home_ref[jnp.clip(entry, 0, n * blocks - 1)]
            rows = gp[stored // blocks, stored % blocks]
            low = j * slot_rows
            kv[low : low + slot_rows, :key_width] = rows[:, :key_width]
            kv[low : low + slot_rows, key_width:] = jnp.where(
                listed, rows[:, key_width:], 0
            ).astype(BF)
            marks[low : low + slot_rows, :] = jnp.where(
                listed, jnp.ones((slot_rows, HEAD_DIM), F32), 0.0
            ).astype(BF)

    def past_part(start, stop, final):
        @pl.loop(start, stop)
        def _(g):
            keys = kv[:, lanes(g * HEAD_DIM)]
            values = jnp.concatenate(
                [kv[:, lanes(key_width + g * HEAD_DIM)], marks[...]], axis=1
            )
            for i in range(GROUP):
                h = g * GROUP + i
                s = lax.dot_general(
                    q_ref[:, lanes(h * HEAD_DIM)], keys, (((1,), (1,)), ((), ())),
                    preferred_element_type=F32,
                )
                before = tops[h]
                top = jnp.maximum(before, wide(jnp.max(s, axis=1, keepdims=True)))
                o = jnp.dot(weights(s, top), values, preferred_element_type=F32)
                shrink = jnp.exp2((before - top) * SCALE)
                total = acc[h, :, :HEAD_DIM] * shrink + o[:, :HEAD_DIM]
                norm = acc[h, :, HEAD_DIM:] * shrink + o[:, HEAD_DIM:]
                if final:
                    attended[:, lanes(h * HEAD_DIM)] = (total / norm).astype(BF)
                else:
                    acc[h, :, :HEAD_DIM] = total
                    acc[h, :, HEAD_DIM:] = norm
                    tops[h] = top

    for piece in past:
        seconds(piece)
    seconds(blocks)
    for piece in past:
        thirds(piece)
    seconds(blocks + 1)
    for piece in past:
        last(piece, 0, inner)
    for c in range(chunks):
        gather_chunk(c)
        final = c == chunks - 1
        if final:
            past_part(0, 1, final)
            thirds(blocks)
            past_part(1, 2, final)
            thirds(blocks + 1)
            past_part(2, 3, final)
            past_part(3, 4, final)
        else:
            past_part(0, KV_HEADS, final)

    last(blocks, 0, inner)
    if gw.shape[1:] == (width, panel):
        for i in range(n):
            wf[:, i * panel : (i + 1) * panel] = gw[i]
    else:
        half = width // 2
        for i in range(0, n, 2):
            for k in (0, 1):
                low = (i + k) * panel
                rest = gw[i + k, width:, :]
                wf[:, low : low + HEAD_DIM] = gw[i + k, :width, :]
                wf[:, low + HEAD_DIM : low + panel] = jnp.concatenate(
                    [rest[:, : panel - HEAD_DIM], rest[:, HEAD_DIM - (panel - HEAD_DIM) :]], axis=0
                )
    predicted = lax.dot_general(
        attended[...], wf[...], (((1,), (1,)), ((), ())), preferred_element_type=F32
    )
    patch_rows = bordered - 2
    predicted = predicted.astype(BF).reshape(frames, patch_rows, patches, width)
    rows_out[0] = predicted[:, patch_rows - 1]
    rows_out[1] = predicted[:, 0]
    pred_ref[:, 1 : bordered - 1] = predicted
    zeros = jnp.zeros((frames, patches, width), BF)

    def exchange(way, target):
        return pltpu.make_async_remote_copy(
            src_ref=rows_out.at[way],
            dst_ref=halo.at[way],
            send_sem=halo_send.at[way],
            recv_sem=halo_recv.at[way],
            device_id={"seq": target},
        )

    @pl.when(me < n - 1)
    def _():
        exchange(0, me + 1).start()

    @pl.when(me > 0)
    def _():
        exchange(1, me - 1).start()

    def window(f, y):
        r, half = (y + 1) // 2, (y + 1) % 2
        piece = pred_ref[f, r].astype(F32)
        for e in range(2):
            low = (2 * half + e) * lat_width
            lat[f, y, pl.ds(8 + e, patches, 2), :] = piece[:, low : low + lat_width]
        rows = jnp.concatenate(
            [lat[f, y, 7 + v : 7 + v + broad, :] for v in range(3)], axis=1
        ).astype(BF)
        for u in range(3):
            for t in range(3):
                if 0 <= y - u < tall and f + 2 - t < frames:
                    low = (3 * t + u) * span
                    taps[f + 2 - t, y - u, :, low : low + span] = rows

    for f in range(frames):
        for y in range(1, tall + 1):
            window(f, y)
    last(blocks + 1, 0, inner)
    for i in range(n):
        wd[i * part : (i + 1) * part, :] = gd[i]

    @pl.when(me > 0)
    def _():
        exchange(0, me - 1).wait_recv()
        pred_ref[:, 0] = halo[0]
        exchange(1, me - 1).wait_send()

    @pl.when(me == 0)
    def _():
        pred_ref[:, 0] = zeros

    @pl.when(me < n - 1)
    def _():
        exchange(1, me + 1).wait_recv()
        pred_ref[:, bordered - 1] = halo[1]
        exchange(0, me + 1).wait_send()

    @pl.when(me == n - 1)
    def _():
        pred_ref[:, bordered - 1] = zeros

    for f in range(frames):
        for y in (0, tall + 1):
            window(f, y)
    for piece in range(pieces):
        for copy in started[piece]:
            copy.wait_send()


def conv_kernel(taps, weight, out_hbm, out, sem):
    frames, tall, broad, taps_all = taps.shape
    channels = weight.shape[0]
    stores = []
    for f in range(frames):
        for y in range(0, tall, ROWS):
            total = lax.dot_general(
                taps[f, y : y + ROWS].reshape(ROWS * broad, taps_all), weight[...],
                (((1,), (1,)), ((), ())), preferred_element_type=F32,
            )
            out[f, y : y + ROWS] = total.astype(BF).reshape(ROWS, broad, channels)
            stores.append(
                pltpu.make_async_copy(
                    out.at[f, y : y + ROWS], out_hbm.at[f, y : y + ROWS], sem.at[len(stores)]
                )
            )
            stores[-1].start()
    for store in stores:
        store.wait()


def local(queries, own_kv, past_kv, block_home, block_list, list_len, final_weight, decoder_weight):
    frames, patch_rows, patches, width_query = queries.shape
    tokens = frames * patch_rows * patches
    n = lax.axis_size("seq")
    inner = 2 if n <= 16 else 16
    outer = n // 2 // inner
    blocks, block_tokens, kv_width = past_kv.shape
    wf_rows, width = final_weight.shape
    taps_all, part = decoder_weight.shape
    vmem = pl.BlockSpec(memory_space=pltpu.VMEM)
    hbm = pl.BlockSpec(memory_space=pltpu.HBM)
    shape = (n, outer, inner, blocks)
    panel = (width, wf_rows)
    if wf_rows == HEAD_DIM + HEAD_DIM // 2 and width % 32 == 0:
        panel = (width + width // 2, HEAD_DIM)
    tall, broad = 2 * patch_rows, 2 * patches
    channels = part * n
    lat_width = width // 4
    taps, weight = pl.pallas_call(
        functools.partial(attend_kernel, shape),
        out_shape=(
            pltpu.VMEM((frames, tall, broad, taps_all), BF),
            pltpu.VMEM((channels, taps_all), BF),
        ),
        in_specs=[hbm] * 8,
        out_specs=(vmem, vmem),
        scratch_shapes=[
            pltpu.VMEM((frames, patch_rows + 2, patches, width), BF),
            pltpu.VMEM((frames, tall + 2, broad + 16, lat_width), F32),
            pltpu.SMEM(block_home.shape, jnp.int32),
            pltpu.SMEM(block_list.shape, jnp.int32),
            pltpu.SMEM(list_len.shape, jnp.int32),
            pltpu.VMEM((tokens, width_query), BF),
            pltpu.VMEM((tokens, kv_width), BF),
            pltpu.VMEM((width, wf_rows), BF),
            pltpu.VMEM((part, taps_all), BF),
            pltpu.VMEM((n, blocks, block_tokens, kv_width), BF),
            pltpu.VMEM((n,) + panel, BF),
            pltpu.VMEM((n, part, taps_all), BF),
            pltpu.VMEM((CHUNK_SLOTS * block_tokens, kv_width), BF),
            pltpu.VMEM((CHUNK_SLOTS * block_tokens, HEAD_DIM), BF),
            pltpu.VMEM((HEADS, tokens, 2 * HEAD_DIM), F32),
            pltpu.VMEM((HEADS, tokens, HEAD_DIM), F32),
            pltpu.VMEM((tokens, width_query), BF),
            pltpu.VMEM((width, width_query), BF),
            pltpu.VMEM((2, frames, patches, width), BF),
            pltpu.VMEM((2, frames, patches, width), BF),
            pltpu.SemaphoreType.DMA((blocks + 2,)),
            pltpu.SemaphoreType.DMA((5,)),
            pltpu.SemaphoreType.DMA((blocks + 2, n)),
            pltpu.SemaphoreType.DMA((blocks + 2, n)),
            pltpu.SemaphoreType.DMA((2,)),
            pltpu.SemaphoreType.DMA((2,)),
        ],
        compiler_params=pltpu.CompilerParams(
            collective_id=0, has_side_effects=True, vmem_limit_bytes=56 << 20
        ),
    )(
        block_home, block_list, list_len,
        queries.reshape(tokens, width_query), own_kv.reshape(tokens, kv_width),
        past_kv, final_weight.T, decoder_weight.T,
    )
    return pl.pallas_call(
        conv_kernel,
        out_shape=jax.ShapeDtypeStruct((frames, tall, broad, channels), BF),
        in_specs=[vmem, vmem],
        out_specs=hbm,
        scratch_shapes=[
            pltpu.VMEM((frames, tall, broad, channels), BF),
            pltpu.SemaphoreType.DMA((frames * tall // ROWS,)),
        ],
        compiler_params=pltpu.CompilerParams(vmem_limit_bytes=24 << 20),
    )(taps, weight)


def solution(mesh):
    return jax.shard_map(
        local,
        mesh=mesh,
        in_specs=(
            P("groups", "seq", None, None),
            P("groups", "seq", None, None),
            P(("groups", "seq"), None, None),
            P("groups"),
            P("groups", None),
            P("groups"),
            P("seq", None),
            P(None, "seq"),
        ),
        out_specs=P("groups", "seq", None, None),
        check_vma=False,
    )
```

```python
import functools
import math

import jax
import jax.numpy as jnp
from jax import lax
from jax.experimental import pallas as pl
from jax.experimental.pallas import tpu as pltpu
from jax.sharding import PartitionSpec as P

HEADS = 24
KV_HEADS = 4
HEAD_DIM = 128
GROUP = HEADS // KV_HEADS
CHUNK_SLOTS = 16
LOG2E = 1.0 / math.log(2.0)
SCALE = LOG2E / math.sqrt(HEAD_DIM)
ROWS = 2
STACK = 3
BF = jnp.bfloat16
F32 = jnp.float32


def attend_kernel(
    shape,
    home_in, list_in, len_in, q_in, own_in, past_ref, final_ref, decoder_ref,
    taps, wd,
    pred_ref, lat, home_ref, list_ref, len_ref, q_ref, own_ref, fin_ref, dcd_ref, gp, gw, gd, kv, marks,
    acc, tops, attended, wf, rows_out, halo,
    load_sem, table_sem, send_sem, recv_sem, halo_send, halo_recv,
):
    n, outer, inner, blocks = shape
    me = lax.axis_index("seq")
    chip, core = me // 2, me % 2
    a, b = chip // inner, chip % inner
    key_width = KV_HEADS * HEAD_DIM
    tokens = q_ref.shape[0]
    slot_rows = gp.shape[2]
    width, panel = fin_ref.shape
    part, taps_all = dcd_ref.shape

    def device(ai, bi, ci):
        return (ai * inner + bi) * 2 + ci

    def across(i):
        if outer & (outer - 1):
            return (a + i) % outer
        at, bit = a, 1
        while bit < outer:
            if i & bit:
                at = at + bit - 2 * bit * ((a // bit) % 2)
            bit *= 2
        return at

    def source(i):
        return (a + outer - i) % outer if outer & (outer - 1) else across(i)

    pieces = blocks + 2

    def held(piece, slot):
        if piece < blocks:
            return gp.at[slot, piece]
        return (gw, gd)[piece - blocks].at[slot]

    loads = [
        pltpu.make_async_copy(past_ref.at[i], gp.at[me, i], load_sem.at[i])
        for i in range(blocks)
    ] + [
        pltpu.make_async_copy(final_ref, fin_ref, load_sem.at[blocks]),
        pltpu.make_async_copy(decoder_ref, dcd_ref, load_sem.at[blocks + 1]),
    ]
    for load in loads:
        load.start()
    tables = [
        pltpu.make_async_copy(ref, held_ref, table_sem.at[i])
        for i, (ref, held_ref) in enumerate(
            (
                (own_in, own_ref), (q_in, q_ref),
                (home_in, home_ref), (list_in, list_ref), (len_in, len_ref),
            )
        )
    ]
    for table in tables:
        table.start()

    partner = device(a, b, 1 - core)
    column = [device(across(i), b, core) for i in range(1, outer)]
    row = [device(a, (b + i) % inner, core) for i in range(1, inner)]
    barrier = pltpu.get_barrier_semaphore()
    around = [(me + 1) % n, (me + n - 1) % n]
    for peer in column + row + [partner] + around:
        pl.semaphore_signal(barrier, inc=1, device_id={"seq": peer})

    pl.semaphore_wait(barrier, outer + inner + 1)

    started = [[] for _ in range(pieces)]

    def send(piece, slot, target):
        copy = pltpu.make_async_remote_copy(
            src_ref=held(piece, slot),
            dst_ref=held(piece, slot),
            send_sem=send_sem.at[piece, len(started[piece])],
            recv_sem=recv_sem.at[piece, slot],
            device_id={"seq": target},
        )
        copy.start()
        started[piece].append(copy)

    def arrived(piece, slot):
        pltpu.make_async_remote_copy(
            src_ref=held(piece, slot),
            dst_ref=held(piece, slot),
            send_sem=send_sem.at[piece, 0],
            recv_sem=recv_sem.at[piece, slot],
            device_id={"seq": partner},
        ).wait_recv()

    def second(piece, i):
        slot = device(source(i), b, core)
        arrived(piece, slot)
        for peer in row:
            send(piece, slot, peer)
        send(piece, slot, partner)

    def third(piece, i):
        at = source(i) if i else a
        for j in range(1, inner):
            slot = device(at, (b + inner - j) % inner, core)
            arrived(piece, slot)
            send(piece, slot, partner)

    def last(piece, first, stop):
        for j in range(first, stop):
            for i in range(outer):
                arrived(piece, device((a + i) % outer, (b + j) % inner, 1 - core))

    past = range(blocks)
    weights_at = (blocks, blocks + 1)
    for piece in past:
        loads[piece].wait()
        for peer in column:
            send(piece, me, peer)
    for piece in past:
        for peer in row:
            send(piece, me, peer)
        send(piece, me, partner)

    def start_row(piece):
        for peer in row:
            send(piece, me, peer)
        send(piece, me, partner)

    def start_column(piece):
        for peer in column:
            send(piece, me, peer)

    def seconds(piece):
        for i in range(1, outer):
            second(piece, i)

    def thirds(piece, first=0):
        for i in range(first, outer):
            third(piece, i)

    loads[blocks].wait()
    loads[blocks + 1].wait()
    if gw.shape[1:] == (width, panel):
        gw[me] = fin_ref[...]
    else:
        gw[me, :width, :] = fin_ref[:, :HEAD_DIM]
        half = width // 2
        gw[me, width:, :] = jnp.concatenate(
            [fin_ref[:half, HEAD_DIM:], fin_ref[half:, HEAD_DIM:]], axis=1
        )
    gd[me] = dcd_ref[...]
    start_row(blocks)
    start_row(blocks + 1)

    def lanes(start):
        return pl.ds(pl.multiple_of(start, HEAD_DIM), HEAD_DIM)

    ones = jnp.ones((tokens, HEAD_DIM), BF)

    def wide(column):
        return jnp.broadcast_to(column, (tokens, HEAD_DIM))

    def weights(s, top):
        return jnp.concatenate(
            [
                jnp.exp2((s[:, i : i + HEAD_DIM] - top) * SCALE).astype(BF)
                for i in range(0, s.shape[1], HEAD_DIM)
            ],
            axis=1,
        )

    def own_part(start, stop):
        @pl.loop(start, stop)
        def _(g):
            keys = own_ref[:, lanes(g * HEAD_DIM)]
            values = jnp.concatenate(
                [own_ref[:, lanes(key_width + g * HEAD_DIM)], ones], axis=1
            )
            for i in range(GROUP):
                h = g * GROUP + i
                s = lax.dot_general(
                    q_ref[:, lanes(h * HEAD_DIM)], keys, (((1,), (1,)), ((), ())),
                    preferred_element_type=F32,
                )
                top = wide(jnp.max(s, axis=1, keepdims=True))
                acc[h] = jnp.dot(weights(s, top), values, preferred_element_type=F32)
                tops[h] = top

    frames, bordered, patches = pred_ref.shape[:3]
    lat_width = width // 4
    tall, broad = 2 * (bordered - 2), 2 * patches
    span = 3 * lat_width
    for f in range(frames):
        lat[f, :, 0:8, :] = jnp.zeros((tall + 2, 8, lat_width), F32)
        lat[f, :, 8 + broad : 16 + broad, :] = jnp.zeros((tall + 2, 8, lat_width), F32)
        for t in range(3):
            if f + t < 2:
                taps[f, :, :, 3 * t * span : 3 * (t + 1) * span] = jnp.zeros(
                    (tall, broad, 3 * span), BF
                )
    tables[0].wait()
    tables[1].wait()
    own_part(0, KV_HEADS)
    start_column(blocks)
    start_column(blocks + 1)
    for table in tables[2:]:
        table.wait()
    count = len_ref[me]
    chunks = list_ref.shape[1] // CHUNK_SLOTS

    def gather_chunk(c):
        for j in range(CHUNK_SLOTS):
            at = c * CHUNK_SLOTS + j
            listed = at < count
            entry = list_ref[me, jnp.where(listed, at, 0)]
            stored = home_ref[jnp.clip(entry, 0, n * blocks - 1)]
            rows = gp[stored // blocks, stored % blocks]
            low = j * slot_rows
            kv[low : low + slot_rows, :key_width] = rows[:, :key_width]
            kv[low : low + slot_rows, key_width:] = jnp.where(
                listed, rows[:, key_width:], 0
            ).astype(BF)
            marks[low : low + slot_rows, :] = jnp.where(
                listed, jnp.ones((slot_rows, HEAD_DIM), F32), 0.0
            ).astype(BF)

    def past_part(start, stop, final):
        @pl.loop(start, stop)
        def _(g):
            keys = kv[:, lanes(g * HEAD_DIM)]
            values = jnp.concatenate(
                [kv[:, lanes(key_width + g * HEAD_DIM)], marks[...]], axis=1
            )
            for first in range(0, GROUP, STACK):
                heads = [g * GROUP + first + i for i in range(STACK)]
                stacked = jnp.concatenate(
                    [q_ref[:, lanes(h * HEAD_DIM)] for h in heads], axis=0
                )
                scores = lax.dot_general(
                    stacked, keys, (((1,), (1,)), ((), ())), preferred_element_type=F32
                )
                top_of, weight_of = [], []
                for i, h in enumerate(heads):
                    s = scores[i * tokens : (i + 1) * tokens]
                    top = jnp.maximum(tops[h], wide(jnp.max(s, axis=1, keepdims=True)))
                    top_of.append(top)
                    weight_of.append(weights(s, top))
                mixed = jnp.dot(
                    jnp.concatenate(weight_of, axis=0), values, preferred_element_type=F32
                )
                for i, h in enumerate(heads):
                    o = mixed[i * tokens : (i + 1) * tokens]
                    top = top_of[i]
                    shrink = jnp.exp2((tops[h] - top) * SCALE)
                    total = acc[h, :, :HEAD_DIM] * shrink + o[:, :HEAD_DIM]
                    norm = acc[h, :, HEAD_DIM:] * shrink + o[:, HEAD_DIM:]
                    if final:
                        attended[:, lanes(h * HEAD_DIM)] = (total * pl.reciprocal(norm)).astype(BF)
                    else:
                        acc[h, :, :HEAD_DIM] = total
                        acc[h, :, HEAD_DIM:] = norm
                        tops[h] = top

    for piece in past:
        seconds(piece)
    seconds(blocks)
    for piece in past:
        thirds(piece)
    for piece in past:
        last(piece, 0, inner)
    for c in range(chunks):
        gather_chunk(c)
        final = c == chunks - 1
        if final:
            past_part(0, 2, final)
            seconds(blocks + 1)
            thirds(blocks)
            past_part(2, 4, final)
        else:
            past_part(0, KV_HEADS, final)

    last(blocks, 0, inner)
    if gw.shape[1:] == (width, panel):
        for i in range(n):
            wf[:, i * panel : (i + 1) * panel] = gw[i]
    else:
        half = width // 2
        for i in range(0, n, 2):
            for k in (0, 1):
                low = (i + k) * panel
                rest = gw[i + k, width:, :]
                wf[:, low : low + HEAD_DIM] = gw[i + k, :width, :]
                wf[:, low + HEAD_DIM : low + panel] = jnp.concatenate(
                    [rest[:, : panel - HEAD_DIM], rest[:, HEAD_DIM - (panel - HEAD_DIM) :]], axis=0
                )
    predicted = lax.dot_general(
        attended[...], wf[...], (((1,), (1,)), ((), ())), preferred_element_type=F32
    )
    patch_rows = bordered - 2
    predicted = predicted.astype(BF).reshape(frames, patch_rows, patches, width)
    rows_out[0] = predicted[:, patch_rows - 1]
    rows_out[1] = predicted[:, 0]
    pred_ref[:, 1 : bordered - 1] = predicted
    zeros = jnp.zeros((frames, patches, width), BF)

    def exchange(way, target):
        return pltpu.make_async_remote_copy(
            src_ref=rows_out.at[way],
            dst_ref=halo.at[way],
            send_sem=halo_send.at[way],
            recv_sem=halo_recv.at[way],
            device_id={"seq": target},
        )

    @pl.when(me < n - 1)
    def _():
        exchange(0, me + 1).start()

    @pl.when(me > 0)
    def _():
        exchange(1, me - 1).start()

    thirds(blocks + 1)

    def window(f, y):
        r, half = (y + 1) // 2, (y + 1) % 2
        piece = pred_ref[f, r].astype(F32)
        for e in range(2):
            low = (2 * half + e) * lat_width
            lat[f, y, pl.ds(8 + e, patches, 2), :] = piece[:, low : low + lat_width]
        rows = jnp.concatenate(
            [lat[f, y, 7 + v : 7 + v + broad, :] for v in range(3)], axis=1
        ).astype(BF)
        for u in range(3):
            for t in range(3):
                if 0 <= y - u < tall and f + 2 - t < frames:
                    low = (3 * t + u) * span
                    taps[f + 2 - t, y - u, :, low : low + span] = rows

    for f in range(frames):
        for y in range(1, tall + 1):
            window(f, y)
    @pl.when(me > 0)
    def _():
        exchange(0, me - 1).wait_recv()
        pred_ref[:, 0] = halo[0]
        exchange(1, me - 1).wait_send()

    @pl.when(me == 0)
    def _():
        pred_ref[:, 0] = zeros

    @pl.when(me < n - 1)
    def _():
        exchange(1, me + 1).wait_recv()
        pred_ref[:, bordered - 1] = halo[1]
        exchange(0, me + 1).wait_send()

    @pl.when(me == n - 1)
    def _():
        pred_ref[:, bordered - 1] = zeros

    for f in range(frames):
        for y in (0, tall + 1):
            window(f, y)
    last(blocks + 1, 0, inner)
    for i in range(n):
        wd[i * part : (i + 1) * part, :] = gd[i]

    for piece in range(pieces):
        for copy in started[piece]:
            copy.wait_send()


def conv_kernel(taps, weight, out_hbm, out, sem):
    frames, tall, broad, taps_all = taps.shape
    channels = weight.shape[0]
    stores = []
    for f in range(frames):
        for y in range(0, tall, ROWS):
            total = lax.dot_general(
                taps[f, y : y + ROWS].reshape(ROWS * broad, taps_all), weight[...],
                (((1,), (1,)), ((), ())), preferred_element_type=F32,
            )
            out[f, y : y + ROWS] = total.astype(BF).reshape(ROWS, broad, channels)
            stores.append(
                pltpu.make_async_copy(
                    out.at[f, y : y + ROWS], out_hbm.at[f, y : y + ROWS], sem.at[len(stores)]
                )
            )
            stores[-1].start()
    for store in stores:
        store.wait()


def local(queries, own_kv, past_kv, block_home, block_list, list_len, final_weight, decoder_weight):
    frames, patch_rows, patches, width_query = queries.shape
    tokens = frames * patch_rows * patches
    n = lax.axis_size("seq")
    inner = 2 if n <= 16 else 16
    outer = n // 2 // inner
    blocks, block_tokens, kv_width = past_kv.shape
    wf_rows, width = final_weight.shape
    taps_all, part = decoder_weight.shape
    vmem = pl.BlockSpec(memory_space=pltpu.VMEM)
    hbm = pl.BlockSpec(memory_space=pltpu.HBM)
    shape = (n, outer, inner, blocks)
    panel = (width, wf_rows)
    if wf_rows == HEAD_DIM + HEAD_DIM // 2 and width % 32 == 0:
        panel = (width + width // 2, HEAD_DIM)
    tall, broad = 2 * patch_rows, 2 * patches
    channels = part * n
    lat_width = width // 4
    taps, weight = pl.pallas_call(
        functools.partial(attend_kernel, shape),
        out_shape=(
            pltpu.VMEM((frames, tall, broad, taps_all), BF),
            pltpu.VMEM((channels, taps_all), BF),
        ),
        in_specs=[hbm] * 8,
        out_specs=(vmem, vmem),
        scratch_shapes=[
            pltpu.VMEM((frames, patch_rows + 2, patches, width), BF),
            pltpu.VMEM((frames, tall + 2, broad + 16, lat_width), F32),
            pltpu.SMEM(block_home.shape, jnp.int32),
            pltpu.SMEM(block_list.shape, jnp.int32),
            pltpu.SMEM(list_len.shape, jnp.int32),
            pltpu.VMEM((tokens, width_query), BF),
            pltpu.VMEM((tokens, kv_width), BF),
            pltpu.VMEM((width, wf_rows), BF),
            pltpu.VMEM((part, taps_all), BF),
            pltpu.VMEM((n, blocks, block_tokens, kv_width), BF),
            pltpu.VMEM((n,) + panel, BF),
            pltpu.VMEM((n, part, taps_all), BF),
            pltpu.VMEM((CHUNK_SLOTS * block_tokens, kv_width), BF),
            pltpu.VMEM((CHUNK_SLOTS * block_tokens, HEAD_DIM), BF),
            pltpu.VMEM((HEADS, tokens, 2 * HEAD_DIM), F32),
            pltpu.VMEM((HEADS, tokens, HEAD_DIM), F32),
            pltpu.VMEM((tokens, width_query), BF),
            pltpu.VMEM((width, width_query), BF),
            pltpu.VMEM((2, frames, patches, width), BF),
            pltpu.VMEM((2, frames, patches, width), BF),
            pltpu.SemaphoreType.DMA((blocks + 2,)),
            pltpu.SemaphoreType.DMA((5,)),
            pltpu.SemaphoreType.DMA((blocks + 2, n)),
            pltpu.SemaphoreType.DMA((blocks + 2, n)),
            pltpu.SemaphoreType.DMA((2,)),
            pltpu.SemaphoreType.DMA((2,)),
        ],
        compiler_params=pltpu.CompilerParams(
            collective_id=0, has_side_effects=True, vmem_limit_bytes=56 << 20
        ),
    )(
        block_home, block_list, list_len,
        queries.reshape(tokens, width_query), own_kv.reshape(tokens, kv_width),
        past_kv, final_weight.T, decoder_weight.T,
    )
    return pl.pallas_call(
        conv_kernel,
        out_shape=jax.ShapeDtypeStruct((frames, tall, broad, channels), BF),
        in_specs=[vmem, vmem],
        out_specs=hbm,
        scratch_shapes=[
            pltpu.VMEM((frames, tall, broad, channels), BF),
            pltpu.SemaphoreType.DMA((frames * tall // ROWS,)),
        ],
        compiler_params=pltpu.CompilerParams(vmem_limit_bytes=24 << 20),
    )(taps, weight)


def solution(mesh):
    return jax.shard_map(
        local,
        mesh=mesh,
        in_specs=(
            P("groups", "seq", None, None),
            P("groups", "seq", None, None),
            P(("groups", "seq"), None, None),
            P("groups"),
            P("groups", None),
            P("groups"),
            P("seq", None),
            P(None, "seq"),
        ),
        out_specs=P("groups", "seq", None, None),
        check_vma=False,
    )
```

```python
import functools
import math

import jax
import jax.numpy as jnp
from jax import lax
from jax.experimental import pallas as pl
from jax.experimental.pallas import tpu as pltpu
from jax.sharding import PartitionSpec as P

HEADS = 24
KV_HEADS = 4
HEAD_DIM = 128
GROUP = HEADS // KV_HEADS
CHUNK_SLOTS = 16
LOG2E = 1.0 / math.log(2.0)
SCALE = LOG2E / math.sqrt(HEAD_DIM)
ROWS = 2
STACK = 3
BF = jnp.bfloat16
F32 = jnp.float32


def attend_kernel(
    shape,
    home_in, list_in, len_in, q_in, own_in, past_ref, final_ref, decoder_ref,
    taps, wd,
    pred_ref, lat, home_ref, list_ref, len_ref, q_ref, own_ref, fin_ref, dcd_ref, gp, gw, gd, kv, marks,
    acc, tops, attended, wf, rows_out, halo,
    load_sem, table_sem, send_sem, recv_sem, halo_send, halo_recv,
):
    n, outer, inner, blocks = shape
    me = lax.axis_index("seq")
    chip, core = me // 2, me % 2
    a, b = chip // inner, chip % inner
    key_width = KV_HEADS * HEAD_DIM
    tokens = q_ref.shape[0]
    slot_rows = gp.shape[2]
    width, panel = fin_ref.shape
    part, taps_all = dcd_ref.shape

    def device(ai, bi, ci):
        return (ai * inner + bi) * 2 + ci

    def across(i):
        if outer & (outer - 1):
            return (a + i) % outer
        at, bit = a, 1
        while bit < outer:
            if i & bit:
                at = at + bit - 2 * bit * ((a // bit) % 2)
            bit *= 2
        return at

    def source(i):
        return (a + outer - i) % outer if outer & (outer - 1) else across(i)

    pieces = blocks + 2

    def held(piece, slot):
        if piece < blocks:
            return gp.at[slot, piece]
        return (gw, gd)[piece - blocks].at[slot]

    loads = [
        pltpu.make_async_copy(past_ref.at[i], gp.at[me, i], load_sem.at[i])
        for i in range(blocks)
    ] + [
        pltpu.make_async_copy(final_ref, fin_ref, load_sem.at[blocks]),
        pltpu.make_async_copy(decoder_ref, dcd_ref, load_sem.at[blocks + 1]),
    ]
    for load in loads:
        load.start()
    tables = [
        pltpu.make_async_copy(ref, held_ref, table_sem.at[i])
        for i, (ref, held_ref) in enumerate(
            (
                (own_in, own_ref), (q_in, q_ref),
                (home_in, home_ref), (list_in, list_ref), (len_in, len_ref),
            )
        )
    ]
    for table in tables:
        table.start()

    partner = device(a, b, 1 - core)
    column = [device(across(i), b, core) for i in range(1, outer)]
    row = [device(a, (b + i) % inner, core) for i in range(1, inner)]
    barrier = pltpu.get_barrier_semaphore()
    around = [(me + 1) % n, (me + n - 1) % n]
    for peer in column + row + [partner] + around:
        pl.semaphore_signal(barrier, inc=1, device_id={"seq": peer})

    pl.semaphore_wait(barrier, outer + inner + 1)

    started = [[] for _ in range(pieces)]

    def send(piece, slot, target):
        copy = pltpu.make_async_remote_copy(
            src_ref=held(piece, slot),
            dst_ref=held(piece, slot),
            send_sem=send_sem.at[piece, len(started[piece])],
            recv_sem=recv_sem.at[piece, slot],
            device_id={"seq": target},
        )
        copy.start()
        started[piece].append(copy)

    def arrived(piece, slot):
        pltpu.make_async_remote_copy(
            src_ref=held(piece, slot),
            dst_ref=held(piece, slot),
            send_sem=send_sem.at[piece, 0],
            recv_sem=recv_sem.at[piece, slot],
            device_id={"seq": partner},
        ).wait_recv()

    def second(piece, i):
        slot = device(source(i), b, core)
        arrived(piece, slot)
        for peer in row:
            send(piece, slot, peer)
        send(piece, slot, partner)

    def third(piece, i):
        at = source(i) if i else a
        for j in range(1, inner):
            slot = device(at, (b + inner - j) % inner, core)
            arrived(piece, slot)
            send(piece, slot, partner)

    def last(piece, first, stop):
        for j in range(first, stop):
            for i in range(outer):
                arrived(piece, device((a + i) % outer, (b + j) % inner, 1 - core))

    past = range(blocks)
    weights_at = (blocks, blocks + 1)
    for piece in past:
        loads[piece].wait()
        for peer in column:
            send(piece, me, peer)
    for piece in past:
        for peer in row:
            send(piece, me, peer)
        send(piece, me, partner)

    def start_row(piece):
        for peer in row:
            send(piece, me, peer)
        send(piece, me, partner)

    def start_column(piece):
        for peer in column:
            send(piece, me, peer)

    def seconds(piece):
        for i in range(1, outer):
            second(piece, i)

    def thirds(piece, first=0):
        for i in range(first, outer):
            third(piece, i)

    loads[blocks].wait()
    loads[blocks + 1].wait()
    if gw.shape[1:] == (width, panel):
        gw[me] = fin_ref[...]
    else:
        gw[me, :width, :] = fin_ref[:, :HEAD_DIM]
        half = width // 2
        gw[me, width:, :] = jnp.concatenate(
            [fin_ref[:half, HEAD_DIM:], fin_ref[half:, HEAD_DIM:]], axis=1
        )
    gd[me] = dcd_ref[...]
    start_row(blocks)
    start_row(blocks + 1)

    def lanes(start):
        return pl.ds(pl.multiple_of(start, HEAD_DIM), HEAD_DIM)

    ones = jnp.ones((tokens, HEAD_DIM), BF)

    def wide(column):
        return jnp.broadcast_to(column, (tokens, HEAD_DIM))

    def weights(s, top):
        return jnp.concatenate(
            [
                jnp.exp2((s[:, i : i + HEAD_DIM] - top) * SCALE).astype(BF)
                for i in range(0, s.shape[1], HEAD_DIM)
            ],
            axis=1,
        )

    def own_part(start, stop):
        @pl.loop(start, stop)
        def _(g):
            keys = own_ref[:, lanes(g * HEAD_DIM)]
            values = jnp.concatenate(
                [own_ref[:, lanes(key_width + g * HEAD_DIM)], ones], axis=1
            )
            for first in range(0, GROUP, STACK):
                heads = [g * GROUP + first + i for i in range(STACK)]
                stacked = jnp.concatenate(
                    [q_ref[:, lanes(h * HEAD_DIM)] for h in heads], axis=0
                )
                scores = lax.dot_general(
                    stacked, keys, (((1,), (1,)), ((), ())), preferred_element_type=F32
                )
                weight_of = []
                for i, h in enumerate(heads):
                    s = scores[i * tokens : (i + 1) * tokens]
                    top = wide(jnp.max(s, axis=1, keepdims=True))
                    tops[h] = top
                    weight_of.append(weights(s, top))
                mixed = jnp.dot(
                    jnp.concatenate(weight_of, axis=0), values, preferred_element_type=F32
                )
                for i, h in enumerate(heads):
                    acc[h] = mixed[i * tokens : (i + 1) * tokens]

    frames, bordered, patches = pred_ref.shape[:3]
    lat_width = width // 4
    tall, broad = 2 * (bordered - 2), 2 * patches
    span = 3 * lat_width
    for f in range(frames):
        lat[f, :, 0:8, :] = jnp.zeros((tall + 2, 8, lat_width), F32)
        lat[f, :, 8 + broad : 16 + broad, :] = jnp.zeros((tall + 2, 8, lat_width), F32)
        for t in range(3):
            if f + t < 2:
                taps[f, :, :, 3 * t * span : 3 * (t + 1) * span] = jnp.zeros(
                    (tall, broad, 3 * span), BF
                )
    tables[0].wait()
    tables[1].wait()
    own_part(0, 3)
    seconds(0)
    start_column(blocks)
    start_column(blocks + 1)
    own_part(3, KV_HEADS)
    for table in tables[2:]:
        table.wait()
    count = len_ref[me]
    chunks = list_ref.shape[1] // CHUNK_SLOTS

    def gather_chunk(c):
        for j in range(CHUNK_SLOTS):
            at = c * CHUNK_SLOTS + j
            listed = at < count
            entry = list_ref[me, jnp.where(listed, at, 0)]
            stored = home_ref[jnp.clip(entry, 0, n * blocks - 1)]
            rows = gp[stored // blocks, stored % blocks]
            low = j * slot_rows
            kv[low : low + slot_rows, :key_width] = rows[:, :key_width]
            kv[low : low + slot_rows, key_width:] = jnp.where(
                listed, rows[:, key_width:], 0
            ).astype(BF)
            marks[low : low + slot_rows, :] = jnp.where(
                listed, jnp.ones((slot_rows, HEAD_DIM), F32), 0.0
            ).astype(BF)

    def past_part(start, stop, final):
        @pl.loop(start, stop)
        def _(g):
            keys = kv[:, lanes(g * HEAD_DIM)]
            values = jnp.concatenate(
                [kv[:, lanes(key_width + g * HEAD_DIM)], marks[...]], axis=1
            )
            for first in range(0, GROUP, STACK):
                heads = [g * GROUP + first + i for i in range(STACK)]
                stacked = jnp.concatenate(
                    [q_ref[:, lanes(h * HEAD_DIM)] for h in heads], axis=0
                )
                scores = lax.dot_general(
                    stacked, keys, (((1,), (1,)), ((), ())), preferred_element_type=F32
                )
                top_of, weight_of = [], []
                for i, h in enumerate(heads):
                    s = scores[i * tokens : (i + 1) * tokens]
                    top = jnp.maximum(tops[h], wide(jnp.max(s, axis=1, keepdims=True)))
                    top_of.append(top)
                    weight_of.append(weights(s, top))
                mixed = jnp.dot(
                    jnp.concatenate(weight_of, axis=0), values, preferred_element_type=F32
                )
                for i, h in enumerate(heads):
                    o = mixed[i * tokens : (i + 1) * tokens]
                    top = top_of[i]
                    shrink = jnp.exp2((tops[h] - top) * SCALE)
                    total = acc[h, :, :HEAD_DIM] * shrink + o[:, :HEAD_DIM]
                    norm = acc[h, :, HEAD_DIM:] * shrink + o[:, HEAD_DIM:]
                    if final:
                        attended[:, lanes(h * HEAD_DIM)] = (total * pl.reciprocal(norm)).astype(BF)
                    else:
                        acc[h, :, :HEAD_DIM] = total
                        acc[h, :, HEAD_DIM:] = norm
                        tops[h] = top

    for piece in past[1:]:
        seconds(piece)
    seconds(blocks)
    for piece in past:
        thirds(piece)
    for piece in past:
        last(piece, 0, inner)
    for c in range(chunks):
        gather_chunk(c)
        final = c == chunks - 1
        if final:
            past_part(0, 2, final)
            seconds(blocks + 1)
            thirds(blocks)
            past_part(2, 4, final)
        else:
            past_part(0, KV_HEADS, final)

    last(blocks, 0, inner)
    if gw.shape[1:] == (width, panel):
        for i in range(n):
            wf[:, i * panel : (i + 1) * panel] = gw[i]
    else:
        half = width // 2
        for i in range(0, n, 2):
            for k in (0, 1):
                low = (i + k) * panel
                rest = gw[i + k, width:, :]
                wf[:, low : low + HEAD_DIM] = gw[i + k, :width, :]
                wf[:, low + HEAD_DIM : low + panel] = jnp.concatenate(
                    [rest[:, : panel - HEAD_DIM], rest[:, HEAD_DIM - (panel - HEAD_DIM) :]], axis=0
                )
    predicted = lax.dot_general(
        attended[...], wf[...], (((1,), (1,)), ((), ())), preferred_element_type=F32
    )
    patch_rows = bordered - 2
    predicted = predicted.astype(BF).reshape(frames, patch_rows, patches, width)
    rows_out[0] = predicted[:, patch_rows - 1]
    rows_out[1] = predicted[:, 0]
    pred_ref[:, 1 : bordered - 1] = predicted
    zeros = jnp.zeros((frames, patches, width), BF)

    def exchange(way, target):
        return pltpu.make_async_remote_copy(
            src_ref=rows_out.at[way],
            dst_ref=halo.at[way],
            send_sem=halo_send.at[way],
            recv_sem=halo_recv.at[way],
            device_id={"seq": target},
        )

    @pl.when(me < n - 1)
    def _():
        exchange(0, me + 1).start()

    @pl.when(me > 0)
    def _():
        exchange(1, me - 1).start()

    thirds(blocks + 1)

    def window(f, y):
        r, half = (y + 1) // 2, (y + 1) % 2
        piece = pred_ref[f, r].astype(F32)
        for e in range(2):
            low = (2 * half + e) * lat_width
            lat[f, y, pl.ds(8 + e, patches, 2), :] = piece[:, low : low + lat_width]
        rows = jnp.concatenate(
            [lat[f, y, 7 + v : 7 + v + broad, :] for v in range(3)], axis=1
        ).astype(BF)
        for u in range(3):
            for t in range(3):
                if 0 <= y - u < tall and f + 2 - t < frames:
                    low = (3 * t + u) * span
                    taps[f + 2 - t, y - u, :, low : low + span] = rows

    for f in range(frames):
        for y in range(1, tall + 1):
            window(f, y)
    @pl.when(me > 0)
    def _():
        exchange(0, me - 1).wait_recv()
        pred_ref[:, 0] = halo[0]
        exchange(1, me - 1).wait_send()

    @pl.when(me == 0)
    def _():
        pred_ref[:, 0] = zeros

    @pl.when(me < n - 1)
    def _():
        exchange(1, me + 1).wait_recv()
        pred_ref[:, bordered - 1] = halo[1]
        exchange(0, me + 1).wait_send()

    @pl.when(me == n - 1)
    def _():
        pred_ref[:, bordered - 1] = zeros

    for f in range(frames):
        for y in (0, tall + 1):
            window(f, y)
    last(blocks + 1, 0, inner)
    for i in range(n):
        wd[i * part : (i + 1) * part, :] = gd[i]

    for piece in range(pieces):
        for copy in started[piece]:
            copy.wait_send()


def conv_kernel(taps, weight, out_hbm, out, sem):
    frames, tall, broad, taps_all = taps.shape
    channels = weight.shape[0]
    stores = []
    for f in range(frames):
        for y in range(0, tall, ROWS):
            total = lax.dot_general(
                taps[f, y : y + ROWS].reshape(ROWS * broad, taps_all), weight[...],
                (((1,), (1,)), ((), ())), preferred_element_type=F32,
            )
            out[f, y : y + ROWS] = total.astype(BF).reshape(ROWS, broad, channels)
            stores.append(
                pltpu.make_async_copy(
                    out.at[f, y : y + ROWS], out_hbm.at[f, y : y + ROWS], sem.at[len(stores)]
                )
            )
            stores[-1].start()
    for store in stores:
        store.wait()


def local(queries, own_kv, past_kv, block_home, block_list, list_len, final_weight, decoder_weight):
    frames, patch_rows, patches, width_query = queries.shape
    tokens = frames * patch_rows * patches
    n = lax.axis_size("seq")
    inner = 2 if n <= 16 else 16
    outer = n // 2 // inner
    blocks, block_tokens, kv_width = past_kv.shape
    wf_rows, width = final_weight.shape
    taps_all, part = decoder_weight.shape
    vmem = pl.BlockSpec(memory_space=pltpu.VMEM)
    hbm = pl.BlockSpec(memory_space=pltpu.HBM)
    shape = (n, outer, inner, blocks)
    panel = (width, wf_rows)
    if wf_rows == HEAD_DIM + HEAD_DIM // 2 and width % 32 == 0:
        panel = (width + width // 2, HEAD_DIM)
    tall, broad = 2 * patch_rows, 2 * patches
    channels = part * n
    lat_width = width // 4
    taps, weight = pl.pallas_call(
        functools.partial(attend_kernel, shape),
        out_shape=(
            pltpu.VMEM((frames, tall, broad, taps_all), BF),
            pltpu.VMEM((channels, taps_all), BF),
        ),
        in_specs=[hbm] * 8,
        out_specs=(vmem, vmem),
        scratch_shapes=[
            pltpu.VMEM((frames, patch_rows + 2, patches, width), BF),
            pltpu.VMEM((frames, tall + 2, broad + 16, lat_width), F32),
            pltpu.SMEM(block_home.shape, jnp.int32),
            pltpu.SMEM(block_list.shape, jnp.int32),
            pltpu.SMEM(list_len.shape, jnp.int32),
            pltpu.VMEM((tokens, width_query), BF),
            pltpu.VMEM((tokens, kv_width), BF),
            pltpu.VMEM((width, wf_rows), BF),
            pltpu.VMEM((part, taps_all), BF),
            pltpu.VMEM((n, blocks, block_tokens, kv_width), BF),
            pltpu.VMEM((n,) + panel, BF),
            pltpu.VMEM((n, part, taps_all), BF),
            pltpu.VMEM((CHUNK_SLOTS * block_tokens, kv_width), BF),
            pltpu.VMEM((CHUNK_SLOTS * block_tokens, HEAD_DIM), BF),
            pltpu.VMEM((HEADS, tokens, 2 * HEAD_DIM), F32),
            pltpu.VMEM((HEADS, tokens, HEAD_DIM), F32),
            pltpu.VMEM((tokens, width_query), BF),
            pltpu.VMEM((width, width_query), BF),
            pltpu.VMEM((2, frames, patches, width), BF),
            pltpu.VMEM((2, frames, patches, width), BF),
            pltpu.SemaphoreType.DMA((blocks + 2,)),
            pltpu.SemaphoreType.DMA((5,)),
            pltpu.SemaphoreType.DMA((blocks + 2, n)),
            pltpu.SemaphoreType.DMA((blocks + 2, n)),
            pltpu.SemaphoreType.DMA((2,)),
            pltpu.SemaphoreType.DMA((2,)),
        ],
        compiler_params=pltpu.CompilerParams(
            collective_id=0, has_side_effects=True, vmem_limit_bytes=56 << 20
        ),
    )(
        block_home, block_list, list_len,
        queries.reshape(tokens, width_query), own_kv.reshape(tokens, kv_width),
        past_kv, final_weight.T, decoder_weight.T,
    )
    return pl.pallas_call(
        conv_kernel,
        out_shape=jax.ShapeDtypeStruct((frames, tall, broad, channels), BF),
        in_specs=[vmem, vmem],
        out_specs=hbm,
        scratch_shapes=[
            pltpu.VMEM((frames, tall, broad, channels), BF),
            pltpu.SemaphoreType.DMA((frames * tall // ROWS,)),
        ],
        compiler_params=pltpu.CompilerParams(vmem_limit_bytes=24 << 20),
    )(taps, weight)


def solution(mesh):
    return jax.shard_map(
        local,
        mesh=mesh,
        in_specs=(
            P("groups", "seq", None, None),
            P("groups", "seq", None, None),
            P(("groups", "seq"), None, None),
            P("groups"),
            P("groups", None),
            P("groups"),
            P("seq", None),
            P(None, "seq"),
        ),
        out_specs=P("groups", "seq", None, None),
        check_vma=False,
    )
```
